32 devices in a mesh: parts: 1, head: 32 (over z, y, x, core).
Axes of the slice: x: 2, y: 2, z: 4, core: 2. Of those that a mesh axis runs over, the one named last changes fastest.
Arguments:
- queries: bfloat16 [8, 2048, 2048], P('parts', 'head'), may hold values from -6 to 6
- keys: bfloat16 [8, 2048, 2048], P('parts', 'head'), may hold values from -6 to 6
- values: bfloat16 [8, 2048, 2048], P('parts', 'head'), may hold values from -6 to 6
- slot_positions: int32 [8, 2048], P('parts', 'head'), may hold values from 0 to 2047, each once within a row
- counts: int32 [8], P('parts'), may hold values from 16 to 2048, as said below
- timesteps: int32 [8], P('parts'), may hold values from 0 to 999
- labels: int32 [8], P('parts'), may hold values from 0 to 127
- time_weight: bfloat16 [256, 4096], replicated, may hold values from -0.375 to 0.375
- norm_gain: float32 [2048], replicated, may hold values from 0.25 to 1.75
- gate_weight: bfloat16 [2048, 8192], P(None, 'head'), may hold values from -0.125 to 0.125
- up_weight: bfloat16 [2048, 8192], P(None, 'head'), may hold values from -0.125 to 0.125
- down_weight: bfloat16 [8192, 2048], P('head'), may hold values from -0.0625 to 0.0625
- class_weight: bfloat16 [2048, 128], replicated, may hold values from -3 to 3
- class_bias: float32 [128], replicated, may hold values from -5 to 112
Outputs:
- attention: bfloat16 [256, 2048, 64], P(('parts', 'head'))
- guidance: float32 [8, 128, 2048], P('parts', 'head')
The draws below stay inside these ranges and needn't reach their ends.
Inputs may be any that keep to these rules, and one draw needn't show every extreme that they name: `counts`: multiples of 16; in every part one shower has exactly 2048. `slot_positions`: each shower's row is a permutation of 0 to 2047.
All inputs are finite; a program needn't handle non-finite values.
Results may differ from the reference program's by a relative error of at most 0.01.
The reference program's roundings to bfloat16 on the way count: a program that leaves them out, or rounds other values in their place, can miss the bound.
Values may be sent and summed in bfloat16 or wider, within the bound.
A program may use at most 192 MiB of HBM per device.

```python
import math
import jax
import jax.numpy as jnp
from jax import lax

HEADS = 32
HD = 64
CD = 2048
FF = 8192
L = 2048
SH = 8
POOL = 16
FREQ = 256
NT = 1000
CLASSES = 128
PAIRS = 256
WP = 128
ROWS = 1024


def drawn_fields(key):
    field_shape = (SH, L, HEADS * HD)
    query_base = jnp.clip(jax.random.normal(jax.random.fold_in(key, 11), field_shape, jnp.float32), -6.0, 6.0)
    key_base = jnp.clip(jax.random.normal(jax.random.fold_in(key, 12), field_shape, jnp.float32), -6.0, 6.0)
    return (query_base, key_base)


def draw_queries(key, part):
    return drawn_fields(key)[0].astype(jnp.bfloat16)


def draw_keys(key, part):
    return drawn_fields(key)[1].astype(jnp.bfloat16)


def draw_counts(key, part):
    units = jax.random.randint(jax.random.fold_in(key, 21), (SH,), 1, L // POOL + 1)
    fullest = jax.random.randint(jax.random.fold_in(key, 22), (), 0, SH)
    units = jnp.where(jnp.arange(SH) == fullest, L // POOL, units)
    return (units * POOL).astype(jnp.int32)


def draw_class_bias(key, part):
    biases = jnp.clip(jax.random.normal(jax.random.fold_in(key, 31), (CLASSES,), jnp.float32), -5.0, 5.0)
    return biases


def touch_ends(result, key, least, top_value):
    extent = result.shape
    index_at = [jax.random.randint(jax.random.fold_in(key, axis), (), 0, extent[axis]) for axis in range(len(extent))]
    result = result.at[tuple(index_at)].set(least)
    longest = extent.index(max(extent))
    index_at[longest] = (index_at[longest] + 1) % extent[longest]
    return result.at[tuple(index_at)].set(top_value)


def level_of(own_key, extent, cuts, smallest, top_value):
    def one(position, parts):
        draws = jax.random.uniform(jax.random.fold_in(jax.random.fold_in(own_key, 6), position), (parts,), jnp.float32, smallest / len(cuts), top_value / len(cuts))
        return jnp.repeat(jnp.exp(draws), extent[position] // parts).reshape((-1,) + (1,) * (len(extent) - position - 1))

    level = one(*cuts[0])
    for cut in cuts[1:]:
        level = level * one(*cut)
    return level


def scatter_about(key, dims, deviation, limit, pieces=(), kind=jnp.bfloat16):
    values = deviation * jax.random.normal(key, dims, jnp.float32)
    if pieces:
        values = values * level_of(key, dims, pieces, -0.22, 0.18)
    return jnp.clip(values, -limit, limit).astype(kind)


def setup_inputs(seed: int = 0, part: int = 0) -> dict:
    seeds = jax.random.split(jax.random.key(seed), 15)
    part_splits = jax.random.split(jax.random.fold_in(seeds[14], part), 15)
    queries = draw_queries(jax.random.fold_in(jax.random.fold_in(seeds[14], part), 71), part)
    keys = draw_keys(jax.random.fold_in(jax.random.fold_in(seeds[14], part), 71), part)
    values = scatter_about(part_splits[2], (SH, L, CD), 1.0, 6.0, ((1, 32),))
    slot_positions = jax.vmap(lambda own: jax.random.permutation(own, L))(jax.random.split(part_splits[3], SH)).reshape((SH, L)).astype(jnp.int32)
    counts = draw_counts(jax.random.fold_in(jax.random.fold_in(seeds[14], part), 71), part)
    timesteps = touch_ends(jax.random.randint(part_splits[5], (SH,), 0, NT), jax.random.fold_in(part_splits[5], 1), 0, NT - 1).astype(jnp.int32)
    labels = touch_ends(jax.random.randint(part_splits[6], (SH,), 0, CLASSES), jax.random.fold_in(part_splits[6], 1), 0, CLASSES - 1).astype(jnp.int32)
    time_weight = scatter_about(seeds[7], (FREQ, 2 * CD), FREQ ** -0.5, 0.375)
    norm_gain = jnp.clip(1.0 + 0.15 * jax.random.normal(seeds[8], (CD,), jnp.float32), 0.25, 1.75)
    gate_weight = scatter_about(seeds[9], (CD, FF), CD ** -0.5, 0.125, ((1, 32),))
    up_weight = scatter_about(seeds[10], (CD, FF), CD ** -0.5, 0.125, ((1, 32),))
    down_weight = scatter_about(seeds[11], (FF, CD), FF ** -0.5, 0.0625, ((0, 32),))
    class_weight = scatter_about(seeds[12], (CD, CLASSES), 0.5, 3.0)
    class_bias = draw_class_bias(jax.random.fold_in(seeds[14], 71), part)
    return {"queries": queries, "keys": keys, "values": values, "slot_positions": slot_positions, "counts": counts, "timesteps": timesteps, "labels": labels, "time_weight": time_weight, "norm_gain": norm_gain, "gate_weight": gate_weight, "up_weight": up_weight, "down_weight": down_weight, "class_weight": class_weight, "class_bias": class_bias}


epsilon = 1e-06

def sinusoid(steps):
    half_width = FREQ // 2
    frequency = jnp.exp(-math.log(10000.0) * jnp.arange(half_width, dtype=jnp.float32) / half_width)
    angles = steps.astype(jnp.float32)[:, None] * frequency[None, :]
    return jnp.concatenate([jnp.cos(angles), jnp.sin(angles)], axis=1)

def to_pairs(block):
    return block.reshape(SH, L, HEADS, HD).transpose(0, 2, 1, 3).reshape(PAIRS, L, HD)

def attend_pair(pair_data):
    query_rows, key_rows, value_rows, key_valid = pair_data
    scores = jnp.dot(query_rows, key_rows.T, preferred_element_type=jnp.float32) * HD ** (-0.5)
    scores = jnp.where(key_valid[None, :], scores, -jnp.inf)
    peak = lax.optimization_barrier(jnp.max(scores, axis=1, keepdims=True))
    exponent = jnp.exp(scores - peak)
    weights = (exponent / lax.optimization_barrier(jnp.sum(exponent, axis=1, keepdims=True))).astype(jnp.bfloat16)
    mixed = jnp.dot(weights, value_rows, preferred_element_type=jnp.float32)
    return (mixed * key_valid[:, None].astype(jnp.float32)).astype(jnp.bfloat16)

def reference(queries, keys, values, slot_positions, counts, timesteps, labels, time_weight, norm_gain, gate_weight, up_weight, down_weight, class_weight, class_bias):
    valid_slots = slot_positions < counts[:, None]
    pair_valid = jnp.repeat(valid_slots, HEADS, axis=0)
    attention = lax.map(attend_pair, (to_pairs(queries), to_pairs(keys), to_pairs(values), pair_valid))
    slot_flags = pair_valid.astype(jnp.float32)
    window_count = lax.optimization_barrier(jnp.sum(slot_flags.reshape(PAIRS, WP, POOL), axis=2))
    window_sum = lax.optimization_barrier(jnp.sum(attention.astype(jnp.float32).reshape(PAIRS, WP, POOL, HD), axis=2))
    pooled = (window_sum / jnp.maximum(window_count, 1.0)[:, :, None]).astype(jnp.bfloat16)
    pooled_rows = pooled.reshape(SH, HEADS, WP, HD).transpose(0, 2, 1, 3).reshape(SH, WP, CD).astype(jnp.float32)
    row_count = window_count.reshape(SH, HEADS, WP)[:, 0, :]
    embedding = sinusoid(timesteps).astype(jnp.bfloat16)
    modulation = jnp.dot(embedding, time_weight, preferred_element_type=jnp.float32)
    shifts = modulation[:, None, :CD]
    scales = 1.0 + modulation[:, None, CD:]
    inverse_rms = lax.rsqrt(lax.optimization_barrier(jnp.mean(pooled_rows * pooled_rows, axis=2, keepdims=True)) + epsilon)
    unit_rows = pooled_rows * inverse_rms
    normed = (unit_rows * norm_gain * scales + shifts).astype(jnp.bfloat16).reshape(ROWS, CD)
    gate_out = jnp.dot(normed, gate_weight, preferred_element_type=jnp.float32)
    up_out = jnp.dot(normed, up_weight, preferred_element_type=jnp.float32)
    activated = jax.nn.silu(gate_out)
    hidden = (activated * up_out).astype(jnp.bfloat16)
    mlp_out = jnp.dot(hidden, down_weight, preferred_element_type=jnp.float32).reshape(SH, WP, CD)
    shower_counts = counts.astype(jnp.float32)
    features = lax.optimization_barrier(jnp.sum(row_count[:, :, None] * (pooled_rows + mlp_out), axis=1)) / shower_counts[:, None]
    class_matrix = class_weight.astype(jnp.float32)
    logits = jnp.dot(features, class_matrix, precision=lax.Precision.HIGHEST) + class_bias
    exponent = jnp.exp(logits - lax.optimization_barrier(jnp.max(logits, axis=1, keepdims=True)))
    probability = exponent / lax.optimization_barrier(jnp.sum(exponent, axis=1, keepdims=True))
    target = (labels[:, None] == jnp.arange(CLASSES, dtype=jnp.int32)[None, :]).astype(jnp.float32)
    feature_grad = jnp.dot(target - probability, class_matrix.T, precision=lax.Precision.HIGHEST)
    row_grads = row_count[:, :, None] / shower_counts[:, None, None] * feature_grad[:, None, :]
    hidden_grad = jnp.dot(row_grads.astype(jnp.bfloat16).reshape(ROWS, CD), down_weight.T, preferred_element_type=jnp.float32)
    sigmoid_gate = jax.nn.sigmoid(gate_out)
    gate_grad = (hidden_grad * up_out * sigmoid_gate * (1.0 + gate_out * (1.0 - sigmoid_gate))).astype(jnp.bfloat16)
    up_grad = (hidden_grad * activated).astype(jnp.bfloat16)
    normed_grad = jnp.dot(gate_grad, gate_weight.T, preferred_element_type=jnp.float32) + jnp.dot(up_grad, up_weight.T, preferred_element_type=jnp.float32)
    unit_grad = normed_grad.reshape(SH, WP, CD) * norm_gain * scales
    pooled_grad = inverse_rms * (unit_grad - unit_rows * lax.optimization_barrier(jnp.mean(unit_grad * unit_rows, axis=2, keepdims=True)))
    guidance = WP * (row_grads + pooled_grad)
    return (attention, guidance)
```

```python
import functools
import math

import jax
import jax.numpy as jnp
from jax import lax
from jax.experimental import pallas as pl
from jax.experimental.pallas import tpu as pltpu
from jax.sharding import PartitionSpec as P

HEADS = 32
POOL = 16
QTILE = 256
MESH = pl.DeviceIdType.MESH

epsilon = 1e-06
HIGHEST = lax.Precision.HIGHEST


def sinusoid(steps, embed_width):
    half_width = embed_width // 2
    frequency = jnp.exp(-math.log(10000.0) * jnp.arange(half_width, dtype=jnp.float32) / half_width)
    angles = steps.astype(jnp.float32)[:, None] * frequency[None, :]
    return jnp.concatenate([jnp.cos(angles), jnp.sin(angles)], axis=1)


def greet_all(n, me):
    barrier = pltpu.get_barrier_semaphore()

    def greet(k, carry):
        pl.semaphore_signal(
            barrier, inc=1, device_id={"head": lax.rem(me + k, n)}, device_id_type=MESH
        )
        return carry

    lax.fori_loop(1, n, greet, 0)
    pl.semaphore_wait(barrier, n - 1)


def swap_kernel(n, q, k, v, f, qo, ko, vo, fo, send_sem, recv_sem, own_sem):
    me = lax.axis_index("head")
    showers, rows, width = q.shape
    cols = qo.shape[1]
    groups = width // cols
    fields = ((q, qo), (k, ko), (v, vo))
    greet_all(n, me)

    def block_of(field, dst):
        return field.at[dst // groups, :, pl.ds(pl.multiple_of((dst % groups) * cols, cols), cols)]

    def slot_of(out, src):
        return out.at[pl.ds(pl.multiple_of(src * rows, rows), rows), :]

    own = [
        pltpu.make_async_copy(block_of(a, me), slot_of(o, me), own_sem.at[i])
        for i, (a, o) in enumerate(fields)
    ]
    own.append(pltpu.make_async_copy(f, fo.at[me], own_sem.at[3]))
    for copy in own:
        copy.start()

    def copies(step):
        dst = lax.rem(me + step, n)
        result = [
            pltpu.make_async_remote_copy(
                src_ref=f,
                dst_ref=fo.at[me],
                send_sem=send_sem.at[3, step],
                recv_sem=recv_sem.at[3, step],
                device_id={"head": dst},
                device_id_type=MESH,
            )
        ]
        for i, (a, o) in enumerate(fields):
            result.append(
                pltpu.make_async_remote_copy(
                    src_ref=block_of(a, dst),
                    dst_ref=slot_of(o, me),
                    send_sem=send_sem.at[i, step],
                    recv_sem=recv_sem.at[i, step],
                    device_id={"head": dst},
                    device_id_type=MESH,
                )
            )
        return result

    def begin(step, carry):
        for copy in copies(step):
            copy.start()
        return carry

    def finish(step, carry):
        for copy in copies(step):
            copy.wait()
        return carry

    lax.fori_loop(1, n, begin, 0)
    lax.fori_loop(1, n, finish, 0)
    for copy in own:
        copy.wait()


def swap(n, q, k, v, f, cols):
    rows = q.shape[1]
    field = jax.ShapeDtypeStruct((n * rows, cols), q.dtype)
    return pl.pallas_call(
        functools.partial(swap_kernel, n),
        out_shape=(field, field, field, jax.ShapeDtypeStruct((n,) + f.shape, f.dtype)),
        in_specs=[pl.BlockSpec(memory_space=pl.ANY)] * 4,
        out_specs=[pl.BlockSpec(memory_space=pl.ANY)] * 4,
        scratch_shapes=[
            pltpu.SemaphoreType.DMA((4, n)),
            pltpu.SemaphoreType.DMA((4, n)),
            pltpu.SemaphoreType.DMA((4,)),
        ],
        compiler_params=pltpu.CompilerParams(collective_id=1, has_side_effects=True),
    )(q, k, v, f)


def total_kernel(n, x, out, held, send_sem, recv_sem):
    me = lax.axis_index("head")
    greet_all(n, me)

    def copy_of(step):
        return pltpu.make_async_remote_copy(
            src_ref=x,
            dst_ref=held.at[step],
            send_sem=send_sem.at[step],
            recv_sem=recv_sem.at[step],
            device_id={"head": lax.rem(me + step, n)},
            device_id_type=MESH,
        )

    def begin(step, carry):
        copy_of(step).start()
        return carry

    def finish(step, carry):
        copy_of(step).wait()
        return carry

    held[0] = x[...]
    lax.fori_loop(1, n, begin, 0)
    lax.fori_loop(1, n, finish, 0)
    total = jnp.zeros(out.shape, jnp.float32)
    for source in range(n):
        total = total + held[lax.rem(me - source + n, n)]
    out[...] = total


def total_over(n, x):
    return pl.pallas_call(
        functools.partial(total_kernel, n),
        out_shape=jax.ShapeDtypeStruct(x.shape, jnp.float32),
        in_specs=[pl.BlockSpec(memory_space=pltpu.VMEM)],
        out_specs=pl.BlockSpec(memory_space=pltpu.VMEM),
        scratch_shapes=[
            pltpu.VMEM((n,) + x.shape, jnp.float32),
            pltpu.SemaphoreType.DMA((n,)),
            pltpu.SemaphoreType.DMA((n,)),
        ],
        compiler_params=pltpu.CompilerParams(collective_id=2, has_side_effects=True),
    )(x)


def scatter_plan(n, orders):
    plan = []
    for order in orders:
        stages = []
        kept = list(range(n))
        for position, bit in enumerate(order):
            away = [r for r in kept if (r >> bit) & 1]
            kept = [r for r in kept if not (r >> bit) & 1]
            following = order[position + 1] if position + 1 < len(order) else None
            if following is not None:
                kept.sort(key=lambda r: (1 - ((r >> following) & 1), r))
            away = [r ^ (1 << bit) for r in kept]
            away = [r for r in away]
            stages.append((bit, away, list(kept)))
        plan.append(stages)
    return plan


def reduce_kernel(n, plan, x, out, held, send_sem, recv_sem):
    me = lax.axis_index("head")
    bits = n.bit_length() - 1
    width = x.shape[2] // len(plan)
    bit_of = [(me // (1 << b)) % 2 for b in range(bits)]

    def flipped(r):
        result = me
        for b in range(bits):
            if (r >> b) & 1:
                result = result + (1 << b) * (1 - 2 * bit_of[b])
        return result

    barrier = pltpu.get_barrier_semaphore()
    for b in range(bits):
        pl.semaphore_signal(
            barrier, inc=1, device_id={"head": flipped(1 << b)}, device_id_type=MESH
        )
    pl.semaphore_wait(barrier, bits)

    def copy_of(stream, slot, bit, r):
        columns = pl.ds(stream * width, width)
        return pltpu.make_async_remote_copy(
            src_ref=x.at[flipped(r), :, columns],
            dst_ref=held.at[stream, slot],
            send_sem=send_sem.at[stream, slot],
            recv_sem=recv_sem.at[stream, slot],
            device_id={"head": flipped(1 << bit)},
            device_id_type=MESH,
        )

    stage_count = len(plan[0])
    slots = [0]
    for stage in range(stage_count):
        slots.append(slots[-1] + len(plan[0][stage][1]))
    everything = []
    for i in range(len(plan[0][0][1])):
        for stream, stages in enumerate(plan):
            bit, away, kept = stages[0]
            copy = copy_of(stream, i, bit, away[i])
            copy.start()
            everything.append(copy)
    for stage in range(stage_count):
        for i in range(len(plan[0][stage][1])):
            for stream, stages in enumerate(plan):
                bit, away, kept = stages[stage]
                slot = slots[stage] + i
                copy_of(stream, slot, bit, away[i]).wait_recv()
                columns = pl.ds(stream * width, width)
                chunk = flipped(kept[i])
                value = x[chunk, :, columns].astype(jnp.float32) + held[stream, slot].astype(
                    jnp.float32
                )
                if stage == stage_count - 1:
                    out[:, columns] = value
                    continue
                x[chunk, :, columns] = value.astype(jnp.bfloat16)
                next_bit, next_away, _ = stages[stage + 1]
                if kept[i] in next_away:
                    copy = copy_of(
                        stream,
                        slots[stage + 1] + next_away.index(kept[i]),
                        next_bit,
                        kept[i],
                    )
                    copy.start()
                    everything.append(copy)
    for copy in everything:
        copy.wait_send()


def reduce_kernel_entry(n, plan, x_ref, out, x, held, load_sem, send_sem, recv_sem):
    load = pltpu.make_async_copy(x_ref, x, load_sem)
    load.start()
    load.wait()
    reduce_kernel(n, plan, x, out, held, send_sem, recv_sem)


def reduce_over(n, x, orders):
    plan = scatter_plan(n, orders)
    chunks, rows, columns = x.shape
    streams = len(plan)
    return pl.pallas_call(
        functools.partial(reduce_kernel_entry, n, plan),
        out_shape=jax.ShapeDtypeStruct((rows, columns), jnp.float32),
        in_specs=[pl.BlockSpec(memory_space=pl.ANY)],
        out_specs=pl.BlockSpec(memory_space=pltpu.VMEM),
        scratch_shapes=[
            pltpu.VMEM(x.shape, x.dtype),
            pltpu.VMEM((streams, n, rows, columns // streams), x.dtype),
            pltpu.SemaphoreType.DMA,
            pltpu.SemaphoreType.DMA((streams, n)),
            pltpu.SemaphoreType.DMA((streams, n)),
        ],
        compiler_params=pltpu.CompilerParams(
            collective_id=3, has_side_effects=True, vmem_limit_bytes=40 * 1024 * 1024
        ),
    )(x)


def attend_kernel(head_dim, q_ref, k_ref, v_ref, valid_ref, att_ref, pooled_ref, key_scratch):
    tile = pl.program_id(1)
    lanes = q_ref.shape[1]
    heads = lanes // head_dim
    length = k_ref.shape[0]
    qtile = q_ref.shape[0]
    key_lane = lax.broadcasted_iota(jnp.int32, (length, lanes), 1)
    lane = lax.broadcasted_iota(jnp.int32, (qtile, lanes), 1)

    @pl.when(tile == 0)
    def _():
        bias = jnp.where(valid_ref[...] > 0.5, 0.0, -1e30)
        for h in range(heads):
            spare = ((h + 1) % heads) * head_dim
            key_scratch[h] = jnp.where(
                key_lane == spare, bias, k_ref[...].astype(jnp.float32)
            ).astype(jnp.bfloat16)

    valid = valid_ref[pl.ds(pl.multiple_of(tile * qtile, qtile), qtile), :]
    query = q_ref[...].astype(jnp.float32) * head_dim ** (-0.5)
    mixed = []
    for h in range(heads):
        spare = ((h + 1) % heads) * head_dim
        inside = (lane >= h * head_dim) & (lane < (h + 1) * head_dim)
        own = jnp.where(inside, query, jnp.where(lane == spare, 1.0, 0.0)).astype(jnp.bfloat16)
        scores = lax.dot_general(
            own, key_scratch[h], (((1,), (1,)), ((), ())), preferred_element_type=jnp.float32
        )
        peak = jnp.max(scores, axis=1, keepdims=True)
        exponent = jnp.exp(scores - peak)
        weights = (exponent * (1.0 / jnp.sum(exponent, axis=1, keepdims=True))).astype(
            jnp.bfloat16
        )
        result = jnp.dot(weights, v_ref[...], preferred_element_type=jnp.float32)
        result = result * valid
        mixed.append(result)
        att_ref[h] = result[:, h * head_dim : (h + 1) * head_dim].astype(jnp.bfloat16)
    joined = mixed[0]
    for h in range(1, heads):
        joined = jnp.where(lane >= h * head_dim, mixed[h], joined)
    windows = qtile // POOL
    row = lax.broadcasted_iota(jnp.int32, (windows, qtile), 0)
    slot = lax.broadcasted_iota(jnp.int32, (windows, qtile), 1)
    gather = jnp.where(slot // POOL == row, 1.0, 0.0).astype(jnp.bfloat16)
    sums = jnp.dot(gather, joined.astype(jnp.bfloat16), preferred_element_type=jnp.float32)
    count = jnp.dot(gather, valid.astype(jnp.bfloat16), preferred_element_type=jnp.float32)
    pooled_ref[...] = (sums / jnp.maximum(count, 1.0)).astype(jnp.bfloat16)


def attend(q, k, v, valid, head_dim):
    length, cols = q.shape
    lanes = 2 * head_dim
    heads = cols // head_dim
    qtile = min(QTILE, length)
    return pl.pallas_call(
        functools.partial(attend_kernel, head_dim),
        grid=(cols // lanes, length // qtile),
        out_shape=(
            jax.ShapeDtypeStruct((heads, length, head_dim), jnp.bfloat16),
            jax.ShapeDtypeStruct((length // POOL, cols), jnp.bfloat16),
        ),
        in_specs=[
            pl.BlockSpec((qtile, lanes), lambda p, t: (t, p)),
            pl.BlockSpec((length, lanes), lambda p, t: (0, p)),
            pl.BlockSpec((length, lanes), lambda p, t: (0, p)),
            pl.BlockSpec((length, lanes), lambda p, t: (0, 0)),
        ],
        out_specs=[
            pl.BlockSpec((2, qtile, head_dim), lambda p, t: (p, t, 0)),
            pl.BlockSpec((qtile // POOL, lanes), lambda p, t: (t, p)),
        ],
        scratch_shapes=[pltpu.VMEM((2, length, lanes), jnp.bfloat16)],
        compiler_params=pltpu.CompilerParams(
            dimension_semantics=("arbitrary", "arbitrary"), vmem_limit_bytes=48 * 1024 * 1024
        ),
    )(q, k, v, valid)


def body(
    queries,
    keys,
    values,
    slot_positions,
    counts,
    timesteps,
    labels,
    time_weight,
    norm_gain,
    gate_weight,
    up_weight,
    down_weight,
    class_weight,
    class_bias,
):
    devices = lax.axis_size("head")
    device_index = lax.axis_index("head")
    showers, local_length, model_width = queries.shape
    head_dim = model_width // HEADS
    pairs_here = showers * HEADS // devices
    length = local_length * devices
    windows = length // POOL
    per_device = windows // devices
    row_total = showers * windows
    cols = pairs_here * head_dim
    groups = model_width // cols

    padded = -(-local_length // 128) * 128
    positions = jnp.pad(slot_positions, ((0, 0), (0, padded - local_length)))
    query_rows, key_rows, value_rows, position_rows = swap(
        devices, queries, keys, values, positions, cols
    )
    valid_all = (position_rows[:, :, :local_length] < counts[None, :, None]).astype(jnp.float32)
    own_shower = device_index // groups
    own_valid = lax.dynamic_index_in_dim(valid_all, own_shower, 1, keepdims=False).reshape(length)
    attention, pooled = attend(
        query_rows,
        key_rows,
        value_rows,
        jnp.broadcast_to(own_valid[:, None], (length, 2 * head_dim)),
        head_dim,
    )
    row_count = jnp.sum(valid_all.reshape(devices, showers, per_device, POOL), axis=3)
    pooled_all = lax.all_gather(pooled, "head", axis=0, tiled=False)
    by_shower = (
        pooled_all.reshape(showers, groups, windows, cols)
        .transpose(0, 2, 1, 3)
        .reshape(row_total, model_width)
    )
    row_id = jnp.arange(row_total, dtype=jnp.int32)
    owner = row_id // (showers * per_device)
    shower_of = (row_id // per_device) % showers
    source = shower_of * windows + owner * per_device + row_id % per_device
    order = (source[:, None] == row_id[None, :]).astype(jnp.bfloat16)
    pooled_rows = jnp.dot(order, by_shower, preferred_element_type=jnp.float32)
    in_shower = shower_of[:, None] == jnp.arange(showers, dtype=jnp.int32)[None, :]
    flat_count = row_count.reshape(row_total)
    spread = in_shower.astype(jnp.float32)

    embedding = sinusoid(timesteps, time_weight.shape[0]).astype(jnp.bfloat16)
    modulation = jnp.dot(embedding, time_weight, preferred_element_type=jnp.float32)
    shifts = modulation[None, :, None, :model_width]
    scales = 1.0 + modulation[:, model_width:]
    gains = norm_gain * scales
    inverse_rms = lax.rsqrt(jnp.mean(pooled_rows * pooled_rows, axis=1, keepdims=True) + epsilon)

    def by_row(table):
        wide = jnp.broadcast_to(
            table[None, :, None, :], (devices, showers, per_device, table.shape[1])
        )
        return wide.reshape(row_total, table.shape[1])

    unit_rows = pooled_rows * inverse_rms
    normed = (
        unit_rows * norm_gain * by_row(scales) + by_row(modulation[:, :model_width])
    ).astype(jnp.bfloat16)
    shower_counts = counts.astype(jnp.float32)
    class_matrix = class_weight.astype(jnp.float32)
    target = (
        labels[:, None] == jnp.arange(class_matrix.shape[1], dtype=jnp.int32)[None, :]
    ).astype(jnp.float32)
    gate_out = jnp.dot(normed, gate_weight, preferred_element_type=jnp.float32)
    up_out = jnp.dot(normed, up_weight, preferred_element_type=jnp.float32)
    activated = jax.nn.silu(gate_out)
    hidden = (activated * up_out).astype(jnp.bfloat16)
    weigh = (spread * flat_count[:, None]).astype(jnp.bfloat16)
    hidden_sum = lax.dot_general(
        weigh, hidden, (((0,), (0,)), ((), ())), preferred_element_type=jnp.float32
    )
    pooled_sum = lax.dot_general(
        weigh,
        pooled_rows.astype(jnp.bfloat16),
        (((0,), (0,)), ((), ())),
        preferred_element_type=jnp.float32,
    )
    mlp_sum = jnp.dot(hidden_sum, down_weight.astype(jnp.float32), precision=HIGHEST)
    partial_logits = jnp.dot(mlp_sum, class_matrix, precision=HIGHEST)
    logit_sum = total_over(devices, partial_logits) + jnp.dot(
        pooled_sum, class_matrix, precision=HIGHEST
    )
    logits = logit_sum / shower_counts[:, None] + class_bias
    exponent = jnp.exp(logits - jnp.max(logits, axis=1, keepdims=True))
    probability = exponent / jnp.sum(exponent, axis=1, keepdims=True)
    feature_grad = jnp.dot(target - probability, class_matrix.T, precision=HIGHEST)
    row_share = row_count / shower_counts[None, :, None]
    row_grads = (row_share[:, :, :, None] * feature_grad[None, :, None, :]).reshape(
        row_total, model_width
    )
    hidden_grad = jnp.dot(
        row_grads.astype(jnp.bfloat16), down_weight.T, preferred_element_type=jnp.float32
    )
    sigmoid_gate = jax.nn.sigmoid(gate_out)
    gate_grad = (
        hidden_grad * up_out * sigmoid_gate * (1.0 + gate_out * (1.0 - sigmoid_gate))
    ).astype(jnp.bfloat16)
    up_grad = (hidden_grad * activated).astype(jnp.bfloat16)
    normed_grad = (
        jnp.dot(gate_grad, gate_weight.T, preferred_element_type=jnp.float32)
        + jnp.dot(up_grad, up_weight.T, preferred_element_type=jnp.float32)
    ).astype(jnp.bfloat16)
    bits = devices.bit_length() - 1
    high = list(range(bits - 1, 2, -1))
    rows_here = showers * per_device
    normed_grad = reduce_over(
        devices,
        normed_grad.reshape(devices, rows_here, model_width),
        ([0, 1, 2] + high, [0, 2, 1] + high),
    )

    def own_rows(table):
        return lax.dynamic_slice_in_dim(table, device_index * rows_here, rows_here, 0)

    def shower_rows(table):
        wide = jnp.broadcast_to(table[:, None, :], (showers, per_device, table.shape[1]))
        return wide.reshape(rows_here, table.shape[1])

    own_pooled = own_rows(pooled_rows)
    own_inverse = lax.rsqrt(jnp.mean(own_pooled * own_pooled, axis=1, keepdims=True) + epsilon)
    own_units = own_pooled * own_inverse
    own_share = lax.dynamic_index_in_dim(row_share, device_index, 0, keepdims=False)
    own_row_grads = (own_share[:, :, None] * feature_grad[:, None, :]).reshape(
        rows_here, model_width
    )
    unit_grad = normed_grad * norm_gain * shower_rows(scales)
    pooled_grad = own_inverse * (
        unit_grad - own_units * jnp.mean(unit_grad * own_units, axis=1, keepdims=True)
    )
    guidance = windows * (own_row_grads + pooled_grad)
    return (attention, guidance.reshape(showers, per_device, model_width))


def solution(mesh):
    in_specs = (
        P("parts", "head", None),
        P("parts", "head", None),
        P("parts", "head", None),
        P("parts", "head"),
        P("parts"),
        P("parts"),
        P("parts"),
        P(),
        P(),
        P(None, "head"),
        P(None, "head"),
        P("head", None),
        P(),
        P(),
    )
    out_specs = (P(("parts", "head"), None, None), P("parts", "head", None))
    return jax.shard_map(body, mesh=mesh, in_specs=in_specs, out_specs=out_specs, check_vma=False)
```

```python
import functools
import math

import jax
import jax.numpy as jnp
from jax import lax
from jax.experimental import pallas as pl
from jax.experimental.pallas import tpu as pltpu
from jax.sharding import PartitionSpec as P

HEADS = 32
POOL = 16
QTILE = 256
MESH = pl.DeviceIdType.MESH

epsilon = 1e-06
HIGHEST = lax.Precision.HIGHEST


def sinusoid(steps, embed_width):
    half_width = embed_width // 2
    frequency = jnp.exp(-math.log(10000.0) * jnp.arange(half_width, dtype=jnp.float32) / half_width)
    angles = steps.astype(jnp.float32)[:, None] * frequency[None, :]
    return jnp.concatenate([jnp.cos(angles), jnp.sin(angles)], axis=1)


def greet_all(n, me):
    barrier = pltpu.get_barrier_semaphore()

    def greet(k, carry):
        pl.semaphore_signal(
            barrier, inc=1, device_id={"head": lax.rem(me + k, n)}, device_id_type=MESH
        )
        return carry

    lax.fori_loop(1, n, greet, 0)
    pl.semaphore_wait(barrier, n - 1)


def swap_kernel(n, q, k, v, f, qo, ko, vo, fo, send_sem, recv_sem, own_sem):
    me = lax.axis_index("head")
    showers, rows, width = q.shape
    cols = qo.shape[1]
    groups = width // cols
    fields = ((q, qo), (k, ko), (v, vo))
    greet_all(n, me)

    def block_of(field, dst):
        return field.at[dst // groups, :, pl.ds(pl.multiple_of((dst % groups) * cols, cols), cols)]

    def slot_of(out, src):
        return out.at[pl.ds(pl.multiple_of(src * rows, rows), rows), :]

    own = [
        pltpu.make_async_copy(block_of(a, me), slot_of(o, me), own_sem.at[i])
        for i, (a, o) in enumerate(fields)
    ]
    own.append(pltpu.make_async_copy(f, fo.at[me], own_sem.at[3]))
    for copy in own:
        copy.start()

    def copies(step):
        dst = lax.rem(me + step, n)
        result = [
            pltpu.make_async_remote_copy(
                src_ref=f,
                dst_ref=fo.at[me],
                send_sem=send_sem.at[3, step],
                recv_sem=recv_sem.at[3, step],
                device_id={"head": dst},
                device_id_type=MESH,
            )
        ]
        for i, (a, o) in enumerate(fields):
            result.append(
                pltpu.make_async_remote_copy(
                    src_ref=block_of(a, dst),
                    dst_ref=slot_of(o, me),
                    send_sem=send_sem.at[i, step],
                    recv_sem=recv_sem.at[i, step],
                    device_id={"head": dst},
                    device_id_type=MESH,
                )
            )
        return result

    def begin(step, carry):
        for copy in copies(step):
            copy.start()
        return carry

    def finish(step, carry):
        for copy in copies(step):
            copy.wait()
        return carry

    lax.fori_loop(1, n, begin, 0)
    lax.fori_loop(1, n, finish, 0)
    for copy in own:
        copy.wait()


def swap(n, q, k, v, f, cols):
    rows = q.shape[1]
    field = jax.ShapeDtypeStruct((n * rows, cols), q.dtype)
    return pl.pallas_call(
        functools.partial(swap_kernel, n),
        out_shape=(field, field, field, jax.ShapeDtypeStruct((n,) + f.shape, f.dtype)),
        in_specs=[pl.BlockSpec(memory_space=pl.ANY)] * 4,
        out_specs=[pl.BlockSpec(memory_space=pl.ANY)] * 4,
        scratch_shapes=[
            pltpu.SemaphoreType.DMA((4, n)),
            pltpu.SemaphoreType.DMA((4, n)),
            pltpu.SemaphoreType.DMA((4,)),
        ],
        compiler_params=pltpu.CompilerParams(collective_id=1, has_side_effects=True),
    )(q, k, v, f)


def total_kernel(n, x, out, held, send_sem, recv_sem):
    me = lax.axis_index("head")
    greet_all(n, me)

    def copy_of(step):
        return pltpu.make_async_remote_copy(
            src_ref=x,
            dst_ref=held.at[step],
            send_sem=send_sem.at[step],
            recv_sem=recv_sem.at[step],
            device_id={"head": lax.rem(me + step, n)},
            device_id_type=MESH,
        )

    def begin(step, carry):
        copy_of(step).start()
        return carry

    def finish(step, carry):
        copy_of(step).wait()
        return carry

    held[0] = x[...]
    lax.fori_loop(1, n, begin, 0)
    lax.fori_loop(1, n, finish, 0)
    total = jnp.zeros(out.shape, jnp.float32)
    for source in range(n):
        total = total + held[lax.rem(me - source + n, n)]
    out[...] = total


def total_over(n, x):
    return pl.pallas_call(
        functools.partial(total_kernel, n),
        out_shape=jax.ShapeDtypeStruct(x.shape, jnp.float32),
        in_specs=[pl.BlockSpec(memory_space=pltpu.VMEM)],
        out_specs=pl.BlockSpec(memory_space=pltpu.VMEM),
        scratch_shapes=[
            pltpu.VMEM((n,) + x.shape, jnp.float32),
            pltpu.SemaphoreType.DMA((n,)),
            pltpu.SemaphoreType.DMA((n,)),
        ],
        compiler_params=pltpu.CompilerParams(collective_id=2, has_side_effects=True),
    )(x)


def scatter_plan(n, orders):
    plan = []
    for order in orders:
        stages = []
        kept = list(range(n))
        for position, bit in enumerate(order):
            away = [r for r in kept if (r >> bit) & 1]
            kept = [r for r in kept if not (r >> bit) & 1]
            following = order[position + 1] if position + 1 < len(order) else None
            if following is not None:
                kept.sort(key=lambda r: (1 - ((r >> following) & 1), r))
            away = [r ^ (1 << bit) for r in kept]
            away = [r for r in away]
            stages.append((bit, away, list(kept)))
        plan.append(stages)
    return plan


def reduce_kernel(n, plan, x, out, held, send_sem, recv_sem):
    me = lax.axis_index("head")
    bits = n.bit_length() - 1
    width = x.shape[2] // len(plan)
    bit_of = [(me // (1 << b)) % 2 for b in range(bits)]

    def flipped(r):
        result = me
        for b in range(bits):
            if (r >> b) & 1:
                result = result + (1 << b) * (1 - 2 * bit_of[b])
        return result

    barrier = pltpu.get_barrier_semaphore()
    for b in range(bits):
        pl.semaphore_signal(
            barrier, inc=1, device_id={"head": flipped(1 << b)}, device_id_type=MESH
        )
    pl.semaphore_wait(barrier, bits)

    def copy_of(stream, slot, bit, r):
        columns = pl.ds(stream * width, width)
        return pltpu.make_async_remote_copy(
            src_ref=x.at[flipped(r), :, columns],
            dst_ref=held.at[stream, slot],
            send_sem=send_sem.at[stream, slot],
            recv_sem=recv_sem.at[stream, slot],
            device_id={"head": flipped(1 << bit)},
            device_id_type=MESH,
        )

    stage_count = len(plan[0])
    slots = [0]
    for stage in range(stage_count):
        slots.append(slots[-1] + len(plan[0][stage][1]))
    everything = []
    for i in range(len(plan[0][0][1])):
        for stream, stages in enumerate(plan):
            bit, away, kept = stages[0]
            copy = copy_of(stream, i, bit, away[i])
            copy.start()
            everything.append(copy)
    for stage in range(stage_count):
        for i in range(len(plan[0][stage][1])):
            for stream, stages in enumerate(plan):
                bit, away, kept = stages[stage]
                slot = slots[stage] + i
                copy_of(stream, slot, bit, away[i]).wait_recv()
                columns = pl.ds(stream * width, width)
                chunk = flipped(kept[i])
                value = x[chunk, :, columns].astype(jnp.float32) + held[stream, slot].astype(
                    jnp.float32
                )
                if stage == stage_count - 1:
                    out[:, columns] = value
                    continue
                x[chunk, :, columns] = value.astype(jnp.bfloat16)
                next_bit, next_away, _ = stages[stage + 1]
                if kept[i] in next_away:
                    copy = copy_of(
                        stream,
                        slots[stage + 1] + next_away.index(kept[i]),
                        next_bit,
                        kept[i],
                    )
                    copy.start()
                    everything.append(copy)
    for copy in everything:
        copy.wait_send()


def reduce_kernel_entry(n, plan, x_ref, out, x, held, load_sem, send_sem, recv_sem):
    load = pltpu.make_async_copy(x_ref, x, load_sem)
    load.start()
    load.wait()
    reduce_kernel(n, plan, x, out, held, send_sem, recv_sem)


def reduce_over(n, x, orders):
    plan = scatter_plan(n, orders)
    chunks, rows, columns = x.shape
    streams = len(plan)
    return pl.pallas_call(
        functools.partial(reduce_kernel_entry, n, plan),
        out_shape=jax.ShapeDtypeStruct((rows, columns), jnp.float32),
        in_specs=[pl.BlockSpec(memory_space=pl.ANY)],
        out_specs=pl.BlockSpec(memory_space=pltpu.VMEM),
        scratch_shapes=[
            pltpu.VMEM(x.shape, x.dtype),
            pltpu.VMEM((streams, n, rows, columns // streams), x.dtype),
            pltpu.SemaphoreType.DMA,
            pltpu.SemaphoreType.DMA((streams, n)),
            pltpu.SemaphoreType.DMA((streams, n)),
        ],
        compiler_params=pltpu.CompilerParams(
            collective_id=3, has_side_effects=True, vmem_limit_bytes=40 * 1024 * 1024
        ),
    )(x)


def collect_kernel(n, orders, x, out, own_sem, send_sem, recv_sem):
    me = lax.axis_index("head")
    bits = n.bit_length() - 1
    height = x.shape[0] // len(orders)
    bit_of = [(me // (1 << b)) % 2 for b in range(bits)]

    def flipped(r):
        result = me
        for b in range(bits):
            if (r >> b) & 1:
                result = result + (1 << b) * (1 - 2 * bit_of[b])
        return result

    barrier = pltpu.get_barrier_semaphore()
    for b in range(bits):
        pl.semaphore_signal(
            barrier, inc=1, device_id={"head": flipped(1 << b)}, device_id_type=MESH
        )
    pl.semaphore_wait(barrier, bits)

    own = pltpu.make_async_copy(x, out.at[me], own_sem)
    own.start()
    everything = []

    def copy_of(stream, r, bit):
        rows = pl.ds(stream * height, height)
        return pltpu.make_async_remote_copy(
            src_ref=x.at[rows] if r == 0 else out.at[flipped(r), rows],
            dst_ref=out.at[flipped(r), rows],
            send_sem=send_sem.at[stream, r | (1 << bit)],
            recv_sem=recv_sem.at[stream, r | (1 << bit)],
            device_id={"head": flipped(1 << bit)},
            device_id_type=MESH,
        )

    def pass_on(stream, r, later):
        for bit in later:
            copy = copy_of(stream, r, bit)
            copy.start()
            everything.append(copy)

    for stream, order in enumerate(orders):
        pass_on(stream, 0, order)
    held = [[0] for _ in orders]
    for stage in range(bits):
        for i in range(1 << stage):
            for stream, order in enumerate(orders):
                bit = order[stage]
                r = held[stream][i]
                copy_of(stream, r, bit).wait_recv()
                pass_on(stream, r | (1 << bit), order[stage + 1 :])
        for stream, order in enumerate(orders):
            held[stream] += [r | (1 << order[stage]) for r in held[stream]]
    for copy in everything:
        copy.wait_send()
    own.wait()


def collect_over(n, x, orders):
    return pl.pallas_call(
        functools.partial(collect_kernel, n, orders),
        out_shape=jax.ShapeDtypeStruct((n,) + x.shape, x.dtype),
        in_specs=[pl.BlockSpec(memory_space=pl.ANY)],
        out_specs=pl.BlockSpec(memory_space=pl.ANY),
        scratch_shapes=[
            pltpu.SemaphoreType.DMA,
            pltpu.SemaphoreType.DMA((len(orders), n)),
            pltpu.SemaphoreType.DMA((len(orders), n)),
        ],
        compiler_params=pltpu.CompilerParams(collective_id=4, has_side_effects=True),
    )(x)


def attend_kernel(head_dim, q_ref, k_ref, v_ref, valid_ref, att_ref, pooled_ref, key_scratch):
    tile = pl.program_id(1)
    lanes = q_ref.shape[1]
    heads = lanes // head_dim
    length = k_ref.shape[0]
    qtile = q_ref.shape[0]
    key_lane = lax.broadcasted_iota(jnp.int32, (length, lanes), 1)
    lane = lax.broadcasted_iota(jnp.int32, (qtile, lanes), 1)

    @pl.when(tile == 0)
    def _():
        bias = jnp.where(valid_ref[...] > 0.5, 0.0, -1e30)
        for h in range(heads):
            spare = ((h + 1) % heads) * head_dim
            key_scratch[h] = jnp.where(
                key_lane == spare, bias, k_ref[...].astype(jnp.float32)
            ).astype(jnp.bfloat16)

    valid = valid_ref[pl.ds(pl.multiple_of(tile * qtile, qtile), qtile), :]
    query = q_ref[...].astype(jnp.float32) * head_dim ** (-0.5)
    mixed = []
    for h in range(heads):
        spare = ((h + 1) % heads) * head_dim
        inside = (lane >= h * head_dim) & (lane < (h + 1) * head_dim)
        own = jnp.where(inside, query, jnp.where(lane == spare, 1.0, 0.0)).astype(jnp.bfloat16)
        scores = lax.dot_general(
            own, key_scratch[h], (((1,), (1,)), ((), ())), preferred_element_type=jnp.float32
        )
        peak = jnp.max(scores, axis=1, keepdims=True)
        exponent = jnp.exp(scores - peak)
        weights = (exponent * (1.0 / jnp.sum(exponent, axis=1, keepdims=True))).astype(
            jnp.bfloat16
        )
        result = jnp.dot(weights, v_ref[...], preferred_element_type=jnp.float32)
        result = result * valid
        mixed.append(result)
    joined = mixed[0]
    for h in range(1, heads):
        joined = jnp.where(lane >= h * head_dim, mixed[h], joined)
    turned = joined.T.astype(jnp.bfloat16)
    for h in range(heads):
        att_ref[h] = turned[h * head_dim : (h + 1) * head_dim, :]
    windows = qtile // POOL
    row = lax.broadcasted_iota(jnp.int32, (windows, qtile), 0)
    slot = lax.broadcasted_iota(jnp.int32, (windows, qtile), 1)
    gather = jnp.where(slot // POOL == row, 1.0, 0.0).astype(jnp.bfloat16)
    sums = jnp.dot(gather, joined.astype(jnp.bfloat16), preferred_element_type=jnp.float32)
    count = jnp.dot(gather, valid.astype(jnp.bfloat16), preferred_element_type=jnp.float32)
    pooled_ref[...] = (sums / jnp.maximum(count, 1.0)).astype(jnp.bfloat16)


def attend(q, k, v, valid, head_dim):
    length, cols = q.shape
    lanes = 2 * head_dim
    heads = cols // head_dim
    qtile = min(QTILE, length)
    return pl.pallas_call(
        functools.partial(attend_kernel, head_dim),
        grid=(cols // lanes, length // qtile),
        out_shape=(
            jax.ShapeDtypeStruct((heads, head_dim, length), jnp.bfloat16),
            jax.ShapeDtypeStruct((length // POOL, cols), jnp.bfloat16),
        ),
        in_specs=[
            pl.BlockSpec((qtile, lanes), lambda p, t: (t, p)),
            pl.BlockSpec((length, lanes), lambda p, t: (0, p)),
            pl.BlockSpec((length, lanes), lambda p, t: (0, p)),
            pl.BlockSpec((length, lanes), lambda p, t: (0, 0)),
        ],
        out_specs=[
            pl.BlockSpec((2, head_dim, qtile), lambda p, t: (p, 0, t)),
            pl.BlockSpec((qtile // POOL, lanes), lambda p, t: (t, p)),
        ],
        scratch_shapes=[pltpu.VMEM((2, length, lanes), jnp.bfloat16)],
        compiler_params=pltpu.CompilerParams(
            dimension_semantics=("arbitrary", "arbitrary"), vmem_limit_bytes=48 * 1024 * 1024
        ),
    )(q, k, v, valid)


def body(
    queries,
    keys,
    values,
    slot_positions,
    counts,
    timesteps,
    labels,
    time_weight,
    norm_gain,
    gate_weight,
    up_weight,
    down_weight,
    class_weight,
    class_bias,
):
    devices = lax.axis_size("head")
    device_index = lax.axis_index("head")
    showers, local_length, model_width = queries.shape
    head_dim = model_width // HEADS
    pairs_here = showers * HEADS // devices
    length = local_length * devices
    windows = length // POOL
    per_device = windows // devices
    row_total = showers * windows
    cols = pairs_here * head_dim
    groups = model_width // cols

    padded = -(-local_length // 128) * 128
    positions = jnp.pad(slot_positions, ((0, 0), (0, padded - local_length)))
    query_rows, key_rows, value_rows, position_rows = swap(
        devices, queries, keys, values, positions, cols
    )
    valid_all = (position_rows[:, :, :local_length] < counts[None, :, None]).astype(jnp.float32)
    own_shower = device_index // groups
    own_valid = lax.dynamic_index_in_dim(valid_all, own_shower, 1, keepdims=False).reshape(length)
    attention, pooled = attend(
        query_rows,
        key_rows,
        value_rows,
        jnp.broadcast_to(own_valid[:, None], (length, 2 * head_dim)),
        head_dim,
    )
    row_count = jnp.sum(valid_all.reshape(devices, showers, per_device, POOL), axis=3)
    bits = devices.bit_length() - 1
    high = list(range(bits - 1, 2, -1))
    pooled_all = collect_over(devices, pooled, (high[::-1] + [2, 1, 0], high[::-1] + [1, 2, 0]))
    by_shower = (
        pooled_all.reshape(showers, groups, windows, cols)
        .transpose(0, 2, 1, 3)
        .reshape(row_total, model_width)
    )
    row_id = jnp.arange(row_total, dtype=jnp.int32)
    owner = row_id // (showers * per_device)
    shower_of = (row_id // per_device) % showers
    source = shower_of * windows + owner * per_device + row_id % per_device
    order = (source[:, None] == row_id[None, :]).astype(jnp.bfloat16)
    pooled_rows = jnp.dot(order, by_shower, preferred_element_type=jnp.float32)
    in_shower = shower_of[:, None] == jnp.arange(showers, dtype=jnp.int32)[None, :]
    flat_count = row_count.reshape(row_total)
    spread = in_shower.astype(jnp.float32)

    embedding = sinusoid(timesteps, time_weight.shape[0]).astype(jnp.bfloat16)
    modulation = jnp.dot(embedding, time_weight, preferred_element_type=jnp.float32)
    shifts = modulation[None, :, None, :model_width]
    scales = 1.0 + modulation[:, model_width:]
    gains = norm_gain * scales
    inverse_rms = lax.rsqrt(jnp.mean(pooled_rows * pooled_rows, axis=1, keepdims=True) + epsilon)

    def by_row(table):
        rows = jnp.broadcast_to(table[:, None, :], (showers, per_device, table.shape[1]))
        rows = lax.optimization_barrier(rows.reshape(1, showers * per_device, table.shape[1]))
        wide = jnp.broadcast_to(rows, (devices,) + rows.shape[1:])
        return wide.reshape(row_total, table.shape[1])

    unit_rows = pooled_rows * inverse_rms
    normed = (
        unit_rows * norm_gain * by_row(scales) + by_row(modulation[:, :model_width])
    ).astype(jnp.bfloat16)
    shower_counts = counts.astype(jnp.float32)
    class_matrix = class_weight.astype(jnp.float32)
    target = (
        labels[:, None] == jnp.arange(class_matrix.shape[1], dtype=jnp.int32)[None, :]
    ).astype(jnp.float32)
    gate_out = jnp.dot(normed, gate_weight, preferred_element_type=jnp.float32)
    up_out = jnp.dot(normed, up_weight, preferred_element_type=jnp.float32)
    activated = jax.nn.silu(gate_out)
    hidden = (activated * up_out).astype(jnp.bfloat16)
    weigh = (spread * flat_count[:, None]).astype(jnp.bfloat16)
    hidden_sum = lax.dot_general(
        weigh, hidden, (((0,), (0,)), ((), ())), preferred_element_type=jnp.float32
    )
    pooled_sum = lax.dot_general(
        weigh,
        pooled_rows.astype(jnp.bfloat16),
        (((0,), (0,)), ((), ())),
        preferred_element_type=jnp.float32,
    )
    mlp_sum = jnp.dot(hidden_sum, down_weight.astype(jnp.float32), precision=HIGHEST)
    partial_logits = jnp.dot(mlp_sum, class_matrix, precision=HIGHEST)
    logit_sum = total_over(devices, partial_logits) + jnp.dot(
        pooled_sum, class_matrix, precision=HIGHEST
    )
    logits = logit_sum / shower_counts[:, None] + class_bias
    exponent = jnp.exp(logits - jnp.max(logits, axis=1, keepdims=True))
    probability = exponent / jnp.sum(exponent, axis=1, keepdims=True)
    feature_grad = jnp.dot(target - probability, class_matrix.T, precision=HIGHEST)
    row_share = row_count / shower_counts[None, :, None]
    row_grads = row_share.reshape(row_total, 1) * by_row(feature_grad)
    hidden_grad = jnp.dot(
        row_grads.astype(jnp.bfloat16), down_weight.T, preferred_element_type=jnp.float32
    )
    sigmoid_gate = jax.nn.sigmoid(gate_out)
    gate_grad = (
        hidden_grad * up_out * sigmoid_gate * (1.0 + gate_out * (1.0 - sigmoid_gate))
    ).astype(jnp.bfloat16)
    up_grad = (hidden_grad * activated).astype(jnp.bfloat16)
    normed_grad = (
        jnp.dot(gate_grad, gate_weight.T, preferred_element_type=jnp.float32)
        + jnp.dot(up_grad, up_weight.T, preferred_element_type=jnp.float32)
    ).astype(jnp.bfloat16)
    rows_here = showers * per_device
    normed_grad = reduce_over(
        devices,
        normed_grad.reshape(devices, rows_here, model_width),
        ([0, 1, 2] + high, [0, 2, 1] + high),
    )

    def own_rows(table):
        return lax.dynamic_slice_in_dim(table, device_index * rows_here, rows_here, 0)

    def shower_rows(table):
        wide = jnp.broadcast_to(table[:, None, :], (showers, per_device, table.shape[1]))
        return wide.reshape(rows_here, table.shape[1])

    own_pooled = own_rows(pooled_rows)
    own_inverse = lax.rsqrt(jnp.mean(own_pooled * own_pooled, axis=1, keepdims=True) + epsilon)
    own_units = own_pooled * own_inverse
    own_share = lax.dynamic_index_in_dim(row_share, device_index, 0, keepdims=False)
    own_row_grads = (own_share[:, :, None] * feature_grad[:, None, :]).reshape(
        rows_here, model_width
    )
    unit_grad = normed_grad * norm_gain * shower_rows(scales)
    pooled_grad = own_inverse * (
        unit_grad - own_units * jnp.mean(unit_grad * own_units, axis=1, keepdims=True)
    )
    guidance = windows * (own_row_grads + pooled_grad)
    return (attention.transpose(0, 2, 1), guidance.reshape(showers, per_device, model_width))


def solution(mesh):
    in_specs = (
        P("parts", "head", None),
        P("parts", "head", None),
        P("parts", "head", None),
        P("parts", "head"),
        P("parts"),
        P("parts"),
        P("parts"),
        P(),
        P(),
        P(None, "head"),
        P(None, "head"),
        P("head", None),
        P(),
        P(),
    )
    out_specs = (P(("parts", "head"), None, None), P("parts", "head", None))
    return jax.shard_map(body, mesh=mesh, in_specs=in_specs, out_specs=out_specs, check_vma=False)
```
